32 devices in a mesh: gz: 8 (over y, x, core), gy: 4 (over z).
Axes of the slice: x: 2, y: 2, z: 4, core: 2. Of those that a mesh axis runs over, the one named last changes fastest.
Arguments:
- velocity: bfloat16 [3, 128, 64, 128], P(None, 'gz', 'gy'), may hold values from -6 to 6
- lag_table: int32 [5, 3], replicated, may hold values from -64 to 64, as said below
- filter_index: int32 [5, 16], replicated, may hold values from 0 to 31
- filter_weights: float32 [3, 32], replicated, may hold values from -4 to 4
Outputs:
- transfer: float32 [128, 64, 128], P('gz', 'gy')
The draws below stay inside these ranges and needn't reach their ends.
Inputs may be any that keep to these rules, and one draw needn't show every extreme that they name: `lag_table`: column 0 is a base x-offset from 0 to 48, column 1 a y lag from -4 to 4, column 2 a z lag from -64 to 64; one lag has z lag exactly 64 and another exactly -64.
All inputs are finite; a program needn't handle non-finite values.
Results may differ from the reference program's by a relative error of at most 0.0004.
Values may be sent and summed in bfloat16 or wider, within the bound.
A program may use at most 64 MiB of HBM per device.

```python
import jax
import jax.numpy as jnp

NX = 128
NLAG = 5
NOFF = 16
REACH = 64
YREACH = 4
NW = 32
NZ = 128
NY = 64


def draw_lag_table(key, part):
    first = jax.random.randint(jax.random.fold_in(key, 11), (NLAG,), 0, 49)
    second = jax.random.randint(jax.random.fold_in(key, 12), (NLAG,), -YREACH, YREACH + 1)
    third = jax.random.randint(jax.random.fold_in(key, 13), (NLAG,), -REACH, REACH + 1)
    order = jax.random.permutation(jax.random.fold_in(key, 14), jnp.arange(NLAG, dtype=jnp.int32))
    slots = jnp.arange(NLAG, dtype=jnp.int32)
    third = jnp.where(slots == order[0], REACH, third)
    third = jnp.where(slots == order[1], -REACH, third)
    return jnp.stack([first, second, third], axis=1).astype(jnp.int32)


def place_ends(array, rng, least, largest):
    longest = array.shape.index(max(array.shape))
    spots = []
    for shift in (0, 1):
        where = [jax.random.randint(jax.random.fold_in(rng, axis), (), 0, length) for axis, length in enumerate(array.shape)]
        where[longest] = (where[longest] + shift) % array.shape[longest]
        spots.append(tuple(where))
    return array.at[spots[0]].set(least).at[spots[1]].set(largest)


def level_of(key, extent, shards, smallest, top_value):
    level = 1.0
    for dim, shards_of in shards:
        heights = jax.random.uniform(jax.random.fold_in(jax.random.fold_in(key, 6), dim), (shards_of,), jnp.float32, smallest / len(shards), top_value / len(shards))
        level = level * jnp.repeat(jnp.exp(heights), extent[dim] // shards_of).reshape((-1,) + (1,) * (len(extent) - 1 - dim))
    return level


def noise(key, shape, scale, reach, split=(), kind=jnp.bfloat16):
    gain = level_of(key, shape, split, -0.22, 0.18) if split else 1.0
    entries = jax.random.normal(key, shape, jnp.float32) * scale * gain
    return jnp.minimum(jnp.maximum(entries, -reach), reach).astype(kind)


def setup_inputs(seed: int = 0) -> dict:
    arg_keys = jax.random.split(jax.random.key(seed), 5)
    velocity = noise(arg_keys[0], (3, NZ, NY, NX), 1.0, 6.0, ((1, 8), (2, 4)))
    lag_table = draw_lag_table(jax.random.fold_in(arg_keys[4], 71), 0)
    filter_index = place_ends(jax.random.randint(arg_keys[2], (NLAG, NOFF), 0, NW), jax.random.fold_in(arg_keys[2], 1), 0, NW - 1).astype(jnp.int32)
    filter_weights = noise(arg_keys[3], (3, NW), 1.0, 4.0, (), jnp.float32)
    return {"velocity": velocity, "lag_table": lag_table, "filter_index": filter_index, "filter_weights": filter_weights}


def reference(velocity, lag_table, filter_index, filter_weights):
    field = velocity.astype(jnp.float32)
    total = jnp.zeros(field.shape[1:], jnp.float32)
    choices_index = jnp.arange(NW, dtype=jnp.int32)
    for lag in range(NLAG):
        base_x = lag_table[lag, 0]
        lag_y = lag_table[lag, 1]
        lag_z = lag_table[lag, 2]
        moved_yz = jnp.roll(field, (-lag_z, -lag_y), axis=(1, 2))
        for offset in range(NOFF):
            moved = jnp.roll(moved_yz, -(base_x + offset), axis=3)
            diff = moved - field
            pick = (choices_index == filter_index[lag, offset]).astype(jnp.float32)
            gradient = jnp.sum(filter_weights * pick[None, :], axis=1)
            along = gradient[0] * diff[0] + gradient[1] * diff[1] + gradient[2] * diff[2]
            energy = diff[0] * diff[0] + diff[1] * diff[1] + diff[2] * diff[2]
            total = total + along * energy
    return total * (0.25 / (NLAG * NOFF))
```

```python
import functools

import jax
import jax.numpy as jnp
from jax import lax
from jax.experimental import pallas as pl
from jax.experimental.pallas import tpu as pltpu
from jax.sharding import PartitionSpec as P

NLAG = 5
NOFF = 16
REACH = 64
TILE = 8
MESH = pl.DeviceIdType.MESH


def kernel(
    pairs, reach, columns, lag_ref, index_ref, weight_ref, vel_ref, out_ref,
    field, base, window, own_sem, send_sem, recv_sem, share_send, share_recv
):
    planes, tiles = vel_ref.shape[1], vel_ref.shape[2]
    length = vel_ref.shape[4]
    slots = field.shape[0]
    last = tiles + 1
    home = reach % pairs
    me = lax.axis_index("gz")
    col = lax.axis_index("gy")
    pair = me // 2
    side = lax.rem(me, 2)
    up = lax.rem(col + 1, columns)
    down = lax.rem(col + columns - 1, columns)
    partner = (pair * 2 + 1 - side, col)
    others = [s for s in range(slots) if s != home]
    others.sort(key=lambda s: -abs(s - reach))

    def peer(slot):
        return (lax.rem(pair + pairs + reach - slot, pairs) * 2 + side, col)

    own = [
        pltpu.make_async_copy(vel_ref.at[:, :, t], field.at[home, side, t + 1], own_sem.at[t])
        for t in range(tiles)
    ]
    for copy in own:
        copy.start()

    barrier = pltpu.get_barrier_semaphore()
    greeted = [peer(s) for s in others] + [partner, (me, up), (me, down)]
    for device in greeted:
        pl.semaphore_signal(barrier, inc=1, device_id=device, device_id_type=MESH)
    pl.semaphore_wait(barrier, len(greeted))

    def direct(src, slot, tile, device):
        return pltpu.make_async_remote_copy(
            src_ref=src,
            dst_ref=field.at[slot, side, tile],
            send_sem=send_sem.at[slot, tile],
            recv_sem=recv_sem.at[slot, tile],
            device_id=device,
            device_id_type=MESH,
        )

    def share(src, slot, tile):
        return pltpu.make_async_remote_copy(
            src_ref=src,
            dst_ref=field.at[slot, side, tile],
            send_sem=share_send.at[slot, tile],
            recv_sem=share_recv.at[slot, tile],
            device_id=partner,
            device_id_type=MESH,
        )

    def incoming(slot, tile):
        return pltpu.make_async_remote_copy(
            src_ref=field.at[slot, 1 - side, tile],
            dst_ref=field.at[slot, 1 - side, tile],
            send_sem=share_send.at[slot, tile],
            recv_sem=share_recv.at[slot, tile],
            device_id=partner,
            device_id_type=MESH,
        )

    started = []

    def go(copy):
        copy.start()
        started.append(copy)
        return copy

    mains = {}
    halos = {}
    for s in others:
        for t in range(tiles):
            mains[s, t] = go(direct(vel_ref.at[:, :, t], s, t + 1, peer(s)))
    halos[home, 0] = go(direct(vel_ref.at[:, :, tiles - 1], home, 0, (me, up)))
    halos[home, last] = go(direct(vel_ref.at[:, :, 0], home, last, (me, down)))
    for t in range(tiles):
        go(share(vel_ref.at[:, :, t], home, t + 1))

    for copy in own:
        copy.wait()

    def fill_base(z, _):
        for c in range(3):
            for t in range(tiles):
                base[c, z, t * TILE:(t + 1) * TILE, :] = field[home, side, t + 1, c, z].astype(jnp.float32)
        for t in range(tiles):
            out_ref[z, t * TILE:(t + 1) * TILE, :] = jnp.zeros((TILE, length), jnp.float32)
        return 0

    lax.fori_loop(0, planes, fill_base, 0)

    def add_lag(lag):
        start = lag_ref[lag, 0]
        lag_y = lag_ref[lag, 1]
        turn = lax.rem(length - start, length)

        def step(z, _):
            spots = [(z * 2 + dz, t) for dz in range(2) for t in range(tiles)]
            centre = [[base[c, zz, t * TILE:(t + 1) * TILE, :] for c in range(3)] for zz, t in spots]
            moved = [
                [
                    pltpu.roll(window[c, zz, pl.ds(TILE + lag_y + t * TILE, TILE), :], turn, 1)
                    for c in range(3)
                ]
                for zz, t in spots
            ]
            total = [out_ref[zz, t * TILE:(t + 1) * TILE, :] for zz, t in spots]
            for k in range(NOFF):
                row = index_ref[lag, k]
                g = [weight_ref[c, row] for c in range(3)]
                for i in range(len(spots)):
                    diff = [
                        (pltpu.roll(moved[i][c], length - k, 1) if k else moved[i][c]) - centre[i][c]
                        for c in range(3)
                    ]
                    along = g[0] * diff[0] + g[1] * diff[1] + g[2] * diff[2]
                    energy = diff[0] * diff[0] + diff[1] * diff[1] + diff[2] * diff[2]
                    total[i] = total[i] + along * energy
            for i, (zz, t) in enumerate(spots):
                out_ref[zz, t * TILE:(t + 1) * TILE, :] = total[i]
            return 0

        lax.fori_loop(0, planes // 2, step, 0)

    def end_lag(lag, slot):
        def load(z, _):
            for c in range(3):
                for t in range(last + 1):
                    window[c, z, t * TILE:(t + 1) * TILE, :] = field[slot, side, t, c, z].astype(jnp.float32)
            return 0

        lax.fori_loop(0, planes, load, 0)
        add_lag(lag)

    def any_lag(lag):
        lag_z = lag_ref[lag, 2]

        def load(z, _):
            away = lag_z + z + 2 * reach * planes
            block = lax.div(away, planes) + side
            plane = lax.rem(away, planes)
            slot = lax.rem(lax.div(block, 2), pairs)
            parity = lax.rem(block, 2)
            for c in range(3):
                for t in range(last + 1):
                    window[c, z, t * TILE:(t + 1) * TILE, :] = field[slot, parity, t, c, plane].astype(jnp.float32)
            return 0

        lax.fori_loop(0, planes, load, 0)
        add_lag(lag)

    for s in others:
        for t in range(tiles):
            mains[s, t].wait_recv()
            if t == 0:
                halos[s, last] = go(direct(field.at[s, side, 1], s, last, (me, down)))
            if t == tiles - 1:
                halos[s, 0] = go(direct(field.at[s, side, tiles], s, 0, (me, up)))
            go(share(field.at[s, side, t + 1], s, t + 1))
        if s == others[0]:
            for edge in (0, last):
                halos[home, edge].wait_recv()
                go(share(field.at[home, side, edge], home, edge))
    for s in others:
        for edge in (last, 0):
            halos[s, edge].wait_recv()
            go(share(field.at[s, side, edge], s, edge))

    plus = jnp.int32(0)
    minus = jnp.int32(0)
    for lag in range(NLAG - 1, -1, -1):
        plus = jnp.where(lag_ref[lag, 2] == REACH, lag, plus)
        minus = jnp.where(lag_ref[lag, 2] == -REACH, lag, minus)
    end_lag(plus, (2 * reach) % pairs)
    end_lag(minus, 0)

    for s in [home] + others:
        for t in range(last + 1):
            incoming(s, t).wait_recv()

    low = jnp.minimum(plus, minus)
    high = jnp.maximum(plus, minus)

    def rest(j, _):
        lag = j + jnp.where(j >= low, 1, 0)
        lag = lag + jnp.where(lag >= high, 1, 0)
        any_lag(lag)
        return 0

    lax.fori_loop(0, NLAG - 2, rest, 0)

    def finish(z, _):
        out_ref[z] = out_ref[z] * (0.25 / (NLAG * NOFF))
        return 0

    lax.fori_loop(0, planes, finish, 0)
    for copy in started:
        copy.wait_send()


def solution(mesh):
    count = mesh.shape["gz"]
    columns = mesh.shape["gy"]
    pairs = count // 2

    def per_device(velocity, lag_table, filter_index, filter_weights):
        parts, planes, rows, length = velocity.shape
        reach = REACH // (2 * planes)
        tiles = rows // TILE
        slots = min(pairs, 2 * reach + 1)
        blocks = velocity.reshape(parts, planes, tiles, TILE, length)
        smem = pl.BlockSpec(memory_space=pltpu.SMEM)
        return pl.pallas_call(
            functools.partial(kernel, pairs, reach, columns),
            out_shape=jax.ShapeDtypeStruct((planes, rows, length), jnp.float32),
            in_specs=[smem, smem, smem, pl.BlockSpec(memory_space=pl.ANY)],
            out_specs=pl.BlockSpec(memory_space=pltpu.VMEM),
            scratch_shapes=[
                pltpu.VMEM((slots, 2, tiles + 2, parts, planes, TILE, length), jnp.bfloat16),
                pltpu.VMEM((parts, planes, rows, length), jnp.float32),
                pltpu.VMEM((parts, planes, rows + 2 * TILE, length), jnp.float32),
                pltpu.SemaphoreType.DMA((tiles,)),
                pltpu.SemaphoreType.DMA((slots, tiles + 2)),
                pltpu.SemaphoreType.DMA((slots, tiles + 2)),
                pltpu.SemaphoreType.DMA((slots, tiles + 2)),
                pltpu.SemaphoreType.DMA((slots, tiles + 2)),
            ],
            compiler_params=pltpu.CompilerParams(collective_id=0, has_side_effects=True),
        )(lag_table, filter_index, filter_weights, blocks)

    return jax.shard_map(
        per_device,
        mesh=mesh,
        in_specs=(P(None, "gz", "gy", None), P(), P(), P()),
        out_specs=P("gz", "gy", None),
        check_vma=False,
    )
```

```python
import functools

import jax
import jax.numpy as jnp
from jax import lax
from jax.experimental import pallas as pl
from jax.experimental.pallas import tpu as pltpu
from jax.sharding import PartitionSpec as P

NLAG = 5
NOFF = 16
REACH = 64
YREACH = 4
MESH = pl.DeviceIdType.MESH


def kernel(
    pairs, reach, columns, lag_ref, index_ref, weight_ref, vel_ref, out_ref,
    field, window, matrix, shifts, own_sem, send_sem, recv_sem, share_send, share_recv
):
    tiles, folded = vel_ref.shape[0], vel_ref.shape[2]
    length = vel_ref.shape[4]
    slots = field.shape[0]
    planes, rows = out_ref.shape[0], out_ref.shape[1]
    fold = planes // folded
    strips = matrix.shape[0]
    deep = planes // strips
    high_rows = deep * rows
    order = [0, tiles - 1] + list(range(1, tiles - 1))
    last = tiles + 1
    home = reach % pairs
    me = lax.axis_index("gz")
    col = lax.axis_index("gy")
    pair = me // 2
    side = lax.rem(me, 2)
    up = lax.rem(col + 1, columns)
    down = lax.rem(col + columns - 1, columns)
    partner = (pair * 2 + 1 - side, col)
    others = [s for s in range(slots) if s != home]
    others.sort(key=lambda s: -abs(s - reach))

    def peer(slot):
        return (lax.rem(pair + pairs + reach - slot, pairs) * 2 + side, col)

    own = [
        pltpu.make_async_copy(vel_ref.at[t], field.at[home, side, t + 1], own_sem.at[t])
        for t in order
    ]
    for copy in own:
        copy.start()

    barrier = pltpu.get_barrier_semaphore()
    greeted = [peer(s) for s in others] + [partner, (me, up), (me, down)]
    for device in greeted:
        pl.semaphore_signal(barrier, inc=1, device_id=device, device_id_type=MESH)
    pl.semaphore_wait(barrier, len(greeted))

    def direct(src, slot, tile, device):
        return pltpu.make_async_remote_copy(
            src_ref=src,
            dst_ref=field.at[slot, side, tile],
            send_sem=send_sem.at[slot, tile],
            recv_sem=recv_sem.at[slot, tile],
            device_id=device,
            device_id_type=MESH,
        )

    def share(src, slot, tile):
        return pltpu.make_async_remote_copy(
            src_ref=src,
            dst_ref=field.at[slot, side, tile],
            send_sem=share_send.at[slot, tile],
            recv_sem=share_recv.at[slot, tile],
            device_id=partner,
            device_id_type=MESH,
        )

    def incoming(slot, tile):
        return pltpu.make_async_remote_copy(
            src_ref=field.at[slot, 1 - side, tile],
            dst_ref=field.at[slot, 1 - side, tile],
            send_sem=share_send.at[slot, tile],
            recv_sem=share_recv.at[slot, tile],
            device_id=partner,
            device_id_type=MESH,
        )

    started = []

    def go(copy):
        copy.start()
        started.append(copy)
        return copy

    mains = {}
    halos = {}
    halos[home, 0] = go(direct(vel_ref.at[tiles - 1], home, 0, (me, up)))
    halos[home, last] = go(direct(vel_ref.at[0], home, last, (me, down)))
    for s in others:
        for t in order:
            mains[s, t] = go(direct(vel_ref.at[t], s, t + 1, peer(s)))
    for t in order:
        go(share(vel_ref.at[t], home, t + 1))

    def build(q, _):
        source = lax.broadcasted_iota(jnp.int32, (length, 2 * length), 0)
        column = lax.broadcasted_iota(jnp.int32, (length, 2 * length), 1)
        point = lax.rem(column, length)
        wanted = lax.rem(point + 2 * q + lax.div(column, length), length)
        shifts[q, :length, :] = jnp.where(source == wanted, 1.0, 0.0).astype(jnp.bfloat16)
        shifts[q, length:, :] = jnp.where(source == point, -1.0, 0.0).astype(jnp.bfloat16)
        return 0

    lax.fori_loop(0, NOFF // 2, build, 0)

    for copy in own:
        copy.wait()

    def unfold(i, tile_of, groups):
        for c in range(3):
            for t in groups:
                tile = tile_of(c, t).astype(jnp.float32)
                for f in range(fold):
                    window[c, fold * i + f, t * YREACH:(t + 1) * YREACH, :] = tile[f * YREACH:(f + 1) * YREACH]

    def fill(lag_y, turn, odd, left):
        def strip(m, _):
            for z in range(deep):
                for c in range(3):
                    block = window[c, m * deep + z + odd, pl.ds(YREACH + lag_y, rows), :]
                    if left:
                        block = pltpu.roll(block, turn, 1)
                    at = c * high_rows + z * rows
                    span = slice(0, length) if left else slice(length, 2 * length)
                    matrix[m, at:at + rows, span] = block.astype(jnp.bfloat16)
            if not left:
                out_ref[pl.ds(m * deep, deep)] = jnp.zeros((deep, rows, length), jnp.float32)
            return 0

        lax.fori_loop(0, strips, strip, 0)

    def unfold_home(i, _):
        unfold(i, lambda c, t: field[home, side, t, c, i], range(1, last))
        return 0

    lax.fori_loop(0, folded, unfold_home, 0)
    fill(0, None, 0, False)

    def add_lag(lag, odd):
        turn = lax.rem(length - lag_ref[0, lag], length)
        fill(lag_ref[1, lag], turn, odd, True)

        def step(m, _):
            total = out_ref[pl.ds(m * deep, deep)].reshape(high_rows, length)
            for q in range(NOFF // 2):
                pieces = jnp.dot(matrix[m], shifts[q], preferred_element_type=jnp.float32)
                for h in range(2):
                    row = index_ref[lag, 2 * q + h]
                    g = [weight_ref[c, row] for c in range(3)]
                    diff = [
                        pieces[c * high_rows:(c + 1) * high_rows, h * length:(h + 1) * length]
                        for c in range(3)
                    ]
                    along = g[0] * diff[0] + g[1] * diff[1] + g[2] * diff[2]
                    energy = diff[0] * diff[0] + diff[1] * diff[1] + diff[2] * diff[2]
                    total = total + along * energy
            out_ref[pl.ds(m * deep, deep)] = total.reshape(deep, rows, length)
            return 0

        lax.fori_loop(0, strips, step, 0)

    def end_lag(lag, slot):
        def load(i, _):
            unfold(i, lambda c, t: field[slot, side, t, c, i], range(last + 1))
            return 0

        lax.fori_loop(0, folded, load, 0)
        add_lag(lag, 0)

    def any_lag(lag):
        away = lag_ref[2, lag] + 2 * reach * planes
        odd = lax.rem(away, fold)
        first = lax.div(away, fold)

        def load(i, _):
            block = lax.div(first + i, folded) + side
            place = lax.rem(first + i, folded)
            slot = lax.rem(lax.div(block, 2), pairs)
            parity = lax.rem(block, 2)
            slot = jnp.minimum(slot, slots - 1)
            unfold(i, lambda c, t: field[slot, parity, t, c, place], range(last + 1))
            return 0

        lax.fori_loop(0, folded + 1, load, 0)
        add_lag(lag, odd)

    for s in others:
        for t in order:
            mains[s, t].wait_recv()
            if t == 0:
                halos[s, last] = go(direct(field.at[s, side, 1], s, last, (me, down)))
            if t == tiles - 1:
                halos[s, 0] = go(direct(field.at[s, side, tiles], s, 0, (me, up)))
            go(share(field.at[s, side, t + 1], s, t + 1))
        if s == others[0]:
            for edge in (0, last):
                halos[home, edge].wait_recv()
                go(share(field.at[home, side, edge], home, edge))
    for s in others:
        for edge in (last, 0):
            halos[s, edge].wait_recv()
            go(share(field.at[s, side, edge], s, edge))

    plus = jnp.int32(0)
    minus = jnp.int32(0)
    for lag in range(NLAG - 1, -1, -1):
        plus = jnp.where(lag_ref[2, lag] == REACH, lag, plus)
        minus = jnp.where(lag_ref[2, lag] == -REACH, lag, minus)
    end_lag(plus, (2 * reach) % pairs)
    end_lag(minus, 0)

    for s in [home] + others:
        for t in range(last + 1):
            incoming(s, t).wait_recv()

    low = jnp.minimum(plus, minus)
    high = jnp.maximum(plus, minus)

    def rest(j, _):
        lag = j + jnp.where(j >= low, 1, 0)
        lag = lag + jnp.where(lag >= high, 1, 0)
        any_lag(lag)
        return 0

    lax.fori_loop(0, NLAG - 2, rest, 0)

    def finish(z, _):
        out_ref[z] = out_ref[z] * (0.25 / (NLAG * NOFF))
        return 0

    lax.fori_loop(0, planes, finish, 0)
    for copy in started:
        copy.wait_send()


def solution(mesh):
    count = mesh.shape["gz"]
    columns = mesh.shape["gy"]
    pairs = count // 2

    def per_device(velocity, lag_table, filter_index, filter_weights):
        parts, planes, rows, length = velocity.shape
        reach = REACH // (2 * planes)
        tiles = rows // YREACH
        fold = 8 // YREACH
        strips = max(1, planes * rows // 64)
        slots = min(pairs, 2 * reach + 1)
        blocks = velocity.reshape(parts, planes // fold, fold, tiles, YREACH, length)
        blocks = blocks.transpose(3, 0, 1, 2, 4, 5).reshape(tiles, parts, planes // fold, 8, length)
        smem = pl.BlockSpec(memory_space=pltpu.SMEM)
        return pl.pallas_call(
            functools.partial(kernel, pairs, reach, columns),
            out_shape=jax.ShapeDtypeStruct((planes, rows, length), jnp.float32),
            in_specs=[smem, smem, smem, pl.BlockSpec(memory_space=pl.ANY)],
            out_specs=pl.BlockSpec(memory_space=pltpu.VMEM),
            scratch_shapes=[
                pltpu.VMEM((slots, 2, tiles + 2, parts, planes // fold, 8, length), jnp.bfloat16),
                pltpu.VMEM((parts, planes + fold, rows + 2 * YREACH, length), jnp.float32),
                pltpu.VMEM((strips, parts * planes * rows // strips, 2 * length), jnp.bfloat16),
                pltpu.VMEM((NOFF // 2, 2 * length, 2 * length), jnp.bfloat16),
                pltpu.SemaphoreType.DMA((tiles,)),
                pltpu.SemaphoreType.DMA((slots, tiles + 2)),
                pltpu.SemaphoreType.DMA((slots, tiles + 2)),
                pltpu.SemaphoreType.DMA((slots, tiles + 2)),
                pltpu.SemaphoreType.DMA((slots, tiles + 2)),
            ],
            compiler_params=pltpu.CompilerParams(collective_id=0, has_side_effects=True),
        )(lag_table.T, filter_index, filter_weights, blocks)

    return jax.shard_map(
        per_device,
        mesh=mesh,
        in_specs=(P(None, "gz", "gy", None), P(), P(), P()),
        out_specs=P("gz", "gy", None),
        check_vma=False,
    )
```

```python
import functools

import jax
import jax.numpy as jnp
from jax import lax
from jax.experimental import pallas as pl
from jax.experimental.pallas import tpu as pltpu
from jax.sharding import PartitionSpec as P

NLAG = 5
NOFF = 16
REACH = 64
YREACH = 4
MESH = pl.DeviceIdType.MESH


def kernel(
    pairs, reach, columns, lag_ref, index_ref, weight_ref, vel_ref, out_ref,
    field, window, matrix, shifts, own_sem, send_sem, recv_sem, share_send, share_recv
):
    planes, tiles = vel_ref.shape[1], vel_ref.shape[2]
    length = vel_ref.shape[4]
    slots = field.shape[0]
    rows = out_ref.shape[1]
    strips = matrix.shape[0]
    deep = planes // strips
    high_rows = deep * rows
    order = [0, tiles - 1] + list(range(1, tiles - 1))
    last = tiles + 1
    me = lax.axis_index("gz")
    col = lax.axis_index("gy")
    pair = me // 2
    side = lax.rem(me, 2)
    up = lax.rem(col + 1, columns)
    down = lax.rem(col + columns - 1, columns)
    partner = (pair * 2 + 1 - side, col)

    paired = slots == pairs and pairs & (pairs - 1) == 0 and reach % pairs in (0, pairs // 2)
    if paired:
        home = 0
        ahead = behind = reach % pairs
        others = sorted(range(1, slots), key=lambda s: (bin(s).count("1"), s != ahead))
        far = [s for s in others if bin(s).count("1") > 1]
    else:
        home, ahead, behind = reach % pairs, (2 * reach) % pairs, 0
        others = sorted((s for s in range(slots) if s != home), key=lambda s: -abs(s - reach))
        far = []
    near = [s for s in others if s not in far]

    def peer(slot):
        if paired:
            other = pair
            for bit in range(pairs.bit_length()):
                if slot >> bit & 1:
                    other = other + (1 << bit) - (2 << bit) * lax.rem(pair // (1 << bit), 2)
        else:
            other = lax.rem(pair + pairs + reach - slot, pairs)
        return (other * 2 + side, col)

    own = [
        pltpu.make_async_copy(vel_ref.at[:, :, t], field.at[home, side, t + 1], own_sem.at[t])
        for t in order
    ]
    for copy in own:
        copy.start()

    barrier = pltpu.get_barrier_semaphore()
    greeted = [peer(s) for s in others] + [partner, (me, up), (me, down)]
    for device in greeted:
        pl.semaphore_signal(barrier, inc=1, device_id=device, device_id_type=MESH)
    pl.semaphore_wait(barrier, len(greeted))

    def direct(src, slot, tile, device):
        return pltpu.make_async_remote_copy(
            src_ref=src,
            dst_ref=field.at[slot, side, tile],
            send_sem=send_sem.at[slot, tile],
            recv_sem=recv_sem.at[slot, tile],
            device_id=device,
            device_id_type=MESH,
        )

    def share(src, slot, tile):
        return pltpu.make_async_remote_copy(
            src_ref=src,
            dst_ref=field.at[slot, side, tile],
            send_sem=share_send.at[slot, tile],
            recv_sem=share_recv.at[slot, tile],
            device_id=partner,
            device_id_type=MESH,
        )

    def incoming(slot, tile):
        return pltpu.make_async_remote_copy(
            src_ref=field.at[slot, 1 - side, tile],
            dst_ref=field.at[slot, 1 - side, tile],
            send_sem=share_send.at[slot, tile],
            recv_sem=share_recv.at[slot, tile],
            device_id=partner,
            device_id_type=MESH,
        )

    started = []

    def go(copy):
        copy.start()
        started.append(copy)
        return copy

    for copy in own:
        copy.wait()
    mains = {}
    halos = {}
    halos[home, 0] = go(direct(field.at[home, side, tiles], home, 0, (me, up)))
    halos[home, last] = go(direct(field.at[home, side, 1], home, last, (me, down)))
    for s in others:
        for t in order:
            mains[s, t] = go(direct(field.at[home, side, t + 1], s, t + 1, peer(s)))
    for t in order:
        go(share(field.at[home, side, t + 1], home, t + 1))

    def build(q, _):
        source = lax.broadcasted_iota(jnp.int32, (length, 2 * length), 0)
        column = lax.broadcasted_iota(jnp.int32, (length, 2 * length), 1)
        point = lax.rem(column, length)
        wanted = lax.rem(point + 2 * q + lax.div(column, length), length)
        shifts[q, :length, :] = jnp.where(source == wanted, 1.0, 0.0).astype(jnp.bfloat16)
        shifts[q, length:, :] = jnp.where(source == point, -1.0, 0.0).astype(jnp.bfloat16)
        return 0

    lax.fori_loop(0, NOFF // 2, build, 0)

    def widen(z, tile_of, groups):
        for c in range(3):
            for t in groups:
                window[c, z, t * YREACH:(t + 1) * YREACH, :] = tile_of(c, t).astype(jnp.float32)

    def fill(lag_y, turn, left):
        def strip(m, _):
            for z in range(deep):
                for c in range(3):
                    block = window[c, m * deep + z, pl.ds(YREACH + lag_y, rows), :]
                    if left:
                        block = pltpu.roll(block, turn, 1)
                    at = c * high_rows + z * rows
                    span = slice(0, length) if left else slice(length, 2 * length)
                    matrix[m, at:at + rows, span] = block.astype(jnp.bfloat16)
            if not left:
                out_ref[pl.ds(m * deep, deep)] = jnp.zeros((deep, rows, length), jnp.float32)
            return 0

        lax.fori_loop(0, strips, strip, 0)

    def widen_home(z, _):
        widen(z, lambda c, t: field[home, side, t, c, z], range(1, last))
        return 0

    lax.fori_loop(0, planes, widen_home, 0)
    fill(0, None, False)

    def add_lag(lag):
        turn = lax.rem(length - lag_ref[0, lag], length)
        fill(lag_ref[1, lag], turn, True)

        def step(m, _):
            total = out_ref[pl.ds(m * deep, deep)].reshape(high_rows, length)
            for q in range(NOFF // 2):
                pieces = jnp.dot(matrix[m], shifts[q], preferred_element_type=jnp.float32)
                for h in range(2):
                    row = index_ref[lag, 2 * q + h]
                    g = [weight_ref[c, row] for c in range(3)]
                    diff = [
                        pieces[c * high_rows:(c + 1) * high_rows, h * length:(h + 1) * length]
                        for c in range(3)
                    ]
                    along = g[0] * diff[0] + g[1] * diff[1] + g[2] * diff[2]
                    energy = diff[0] * diff[0] + diff[1] * diff[1] + diff[2] * diff[2]
                    total = total + along * energy
            out_ref[pl.ds(m * deep, deep)] = total.reshape(deep, rows, length)
            return 0

        lax.fori_loop(0, strips, step, 0)

    def end_lag(lag, slot):
        def load(z, _):
            widen(z, lambda c, t: field[slot, side, t, c, z], range(last + 1))
            return 0

        lax.fori_loop(0, planes, load, 0)
        add_lag(lag)

    def any_lag(lag):
        lag_z = lag_ref[2, lag]

        def load(z, _):
            away = lag_z + z + 2 * reach * planes
            block = lax.div(away, planes) + side
            place = lax.rem(away, planes)
            parity = lax.rem(block, 2)
            if paired:
                slot = lax.rem(pair + lax.div(block, 2) + pairs - reach % pairs, pairs) ^ pair
            else:
                slot = lax.rem(lax.div(block, 2), pairs)
            widen(z, lambda c, t: field[slot, parity, t, c, place], range(last + 1))
            return 0

        lax.fori_loop(0, planes, load, 0)
        add_lag(lag)

    def pass_halo(s, edge):
        halos[s, edge].wait_recv()
        go(share(field.at[s, side, edge], s, edge))

    plus = jnp.int32(0)
    minus = jnp.int32(0)
    for lag in range(NLAG - 1, -1, -1):
        plus = jnp.where(lag_ref[2, lag] == REACH, lag, plus)
        minus = jnp.where(lag_ref[2, lag] == -REACH, lag, minus)

    for edge in (last, 0):
        pass_halo(home, edge)
        for s in far:
            halos[s, edge] = go(direct(field.at[home, side, edge], s, edge, peer(s)))
    for s in near:
        for t in order:
            mains[s, t].wait_recv()
            if t == 0:
                halos[s, last] = go(direct(field.at[s, side, 1], s, last, (me, down)))
            if t == tiles - 1:
                halos[s, 0] = go(direct(field.at[s, side, tiles], s, 0, (me, up)))
            go(share(field.at[s, side, t + 1], s, t + 1))
    first = near[0]
    for edge in (last, 0):
        pass_halo(first, edge)
    if first == ahead:
        end_lag(plus, ahead)
    for s in far:
        for t in order:
            mains[s, t].wait_recv()
            go(share(field.at[s, side, t + 1], s, t + 1))
    for s in near[1:]:
        for edge in (last, 0):
            pass_halo(s, edge)
    if first != ahead:
        end_lag(plus, ahead)
    end_lag(minus, behind)
    for s in far:
        for edge in (last, 0):
            pass_halo(s, edge)
    for s in [home] + others:
        for t in range(last + 1):
            incoming(s, t).wait_recv()

    low = jnp.minimum(plus, minus)
    high = jnp.maximum(plus, minus)

    def rest(j, _):
        lag = j + jnp.where(j >= low, 1, 0)
        lag = lag + jnp.where(lag >= high, 1, 0)
        any_lag(lag)
        return 0

    lax.fori_loop(0, NLAG - 2, rest, 0)

    def finish(z, _):
        out_ref[z] = out_ref[z] * (0.25 / (NLAG * NOFF))
        return 0

    lax.fori_loop(0, planes, finish, 0)
    for copy in started:
        copy.wait_send()


def solution(mesh):
    count = mesh.shape["gz"]
    columns = mesh.shape["gy"]
    pairs = count // 2

    def per_device(velocity, lag_table, filter_index, filter_weights):
        parts, planes, rows, length = velocity.shape
        reach = REACH // (2 * planes)
        tiles = rows // YREACH
        strips = max(1, planes * rows // 64)
        slots = min(pairs, 2 * reach + 1)
        blocks = velocity.reshape(parts, planes, tiles, YREACH, length)
        smem = pl.BlockSpec(memory_space=pltpu.SMEM)
        return pl.pallas_call(
            functools.partial(kernel, pairs, reach, columns),
            out_shape=jax.ShapeDtypeStruct((planes, rows, length), jnp.float32),
            in_specs=[smem, smem, smem, pl.BlockSpec(memory_space=pl.ANY)],
            out_specs=pl.BlockSpec(memory_space=pltpu.VMEM),
            scratch_shapes=[
                pltpu.VMEM((slots, 2, tiles + 2, parts, planes, YREACH, length), jnp.bfloat16),
                pltpu.VMEM((parts, planes, rows + 2 * YREACH, length), jnp.float32),
                pltpu.VMEM((strips, parts * planes * rows // strips, 2 * length), jnp.bfloat16),
                pltpu.VMEM((NOFF // 2, 2 * length, 2 * length), jnp.bfloat16),
                pltpu.SemaphoreType.DMA((tiles,)),
                pltpu.SemaphoreType.DMA((slots, tiles + 2)),
                pltpu.SemaphoreType.DMA((slots, tiles + 2)),
                pltpu.SemaphoreType.DMA((slots, tiles + 2)),
                pltpu.SemaphoreType.DMA((slots, tiles + 2)),
            ],
            compiler_params=pltpu.CompilerParams(collective_id=0, has_side_effects=True),
        )(lag_table.T, filter_index, filter_weights, blocks)

    return jax.shard_map(
        per_device,
        mesh=mesh,
        in_specs=(P(None, "gz", "gy", None), P(), P(), P()),
        out_specs=P("gz", "gy", None),
        check_vma=False,
    )
```

```python
import functools

import jax
import jax.numpy as jnp
from jax import lax
from jax.experimental import pallas as pl
from jax.experimental.pallas import tpu as pltpu
from jax.sharding import PartitionSpec as P

NLAG = 5
NOFF = 16
REACH = 64
YREACH = 4
MESH = pl.DeviceIdType.MESH


def kernel(
    pairs, reach, columns, lag_ref, index_ref, weight_ref, vel_ref, out_ref,
    field, window, matrix, shifts, own_sem, send_sem, recv_sem, share_send, share_recv
):
    planes, tiles = vel_ref.shape[1], vel_ref.shape[2]
    length = vel_ref.shape[4]
    slots = field.shape[0]
    rows = out_ref.shape[1]
    strips = matrix.shape[1]
    deep = planes // strips
    high_rows = deep * rows
    order = [0, tiles - 1] + list(range(1, tiles - 1))
    last = tiles + 1
    me = lax.axis_index("gz")
    col = lax.axis_index("gy")
    pair = me // 2
    side = lax.rem(me, 2)
    up = lax.rem(col + 1, columns)
    down = lax.rem(col + columns - 1, columns)
    partner = (pair * 2 + 1 - side, col)

    paired = slots == pairs and pairs & (pairs - 1) == 0 and reach % pairs in (0, pairs // 2)
    if paired:
        home = 0
        ahead = behind = reach % pairs
        others = sorted(range(1, slots), key=lambda s: (bin(s).count("1"), s != ahead))
        far = [s for s in others if bin(s).count("1") > 1]
    else:
        home, ahead, behind = reach % pairs, (2 * reach) % pairs, 0
        others = sorted((s for s in range(slots) if s != home), key=lambda s: -abs(s - reach))
        far = []
    near = [s for s in others if s not in far]
    relayed = None
    if len(far) == 1 and len(near) == 2:
        relayed = {near[0]: range(tiles // 2), near[1]: range(tiles // 2, tiles)}

    def peer(slot):
        if paired:
            other = pair
            for bit in range(pairs.bit_length()):
                if slot >> bit & 1:
                    other = other + (1 << bit) - (2 << bit) * lax.rem(pair // (1 << bit), 2)
        else:
            other = lax.rem(pair + pairs + reach - slot, pairs)
        return (other * 2 + side, col)

    own = [
        pltpu.make_async_copy(vel_ref.at[:, :, t], field.at[home, side, t + 1], own_sem.at[t])
        for t in order
    ]
    for copy in own:
        copy.start()

    barrier = pltpu.get_barrier_semaphore()
    greeted = [peer(s) for s in others] + [partner, (me, up), (me, down)]
    for device in greeted:
        pl.semaphore_signal(barrier, inc=1, device_id=device, device_id_type=MESH)
    pl.semaphore_wait(barrier, len(greeted))

    def direct(src, slot, tile, device):
        return pltpu.make_async_remote_copy(
            src_ref=src,
            dst_ref=field.at[slot, side, tile],
            send_sem=send_sem.at[slot, tile],
            recv_sem=recv_sem.at[slot, tile],
            device_id=device,
            device_id_type=MESH,
        )

    def share(src, slot, tile):
        return pltpu.make_async_remote_copy(
            src_ref=src,
            dst_ref=field.at[slot, side, tile],
            send_sem=share_send.at[slot, tile],
            recv_sem=share_recv.at[slot, tile],
            device_id=partner,
            device_id_type=MESH,
        )

    def incoming(slot, tile):
        return pltpu.make_async_remote_copy(
            src_ref=field.at[slot, 1 - side, tile],
            dst_ref=field.at[slot, 1 - side, tile],
            send_sem=share_send.at[slot, tile],
            recv_sem=share_recv.at[slot, tile],
            device_id=partner,
            device_id_type=MESH,
        )

    started = []

    def go(copy):
        copy.start()
        started.append(copy)
        return copy

    for copy in own:
        copy.wait()
    mains = {}
    halos = {}
    halos[home, 0] = go(direct(field.at[home, side, tiles], home, 0, (me, up)))
    halos[home, last] = go(direct(field.at[home, side, 1], home, last, (me, down)))
    for t in order:
        for s in near if relayed else others:
            mains[s, t] = go(direct(field.at[home, side, t + 1], s, t + 1, peer(s)))
    for t in order:
        go(share(field.at[home, side, t + 1], home, t + 1))

    def build(q, _):
        source = lax.broadcasted_iota(jnp.int32, (length, 2 * length), 0)
        column = lax.broadcasted_iota(jnp.int32, (length, 2 * length), 1)
        point = lax.rem(column, length)
        wanted = lax.rem(point + 2 * q + lax.div(column, length), length)
        shifts[q, :length, :] = jnp.where(source == wanted, 1.0, 0.0).astype(jnp.bfloat16)
        shifts[q, length:, :] = jnp.where(source == point, -1.0, 0.0).astype(jnp.bfloat16)
        return 0

    lax.fori_loop(0, NOFF // 2, build, 0)

    def widen(z, tile_of, groups):
        for c in range(3):
            for t in groups:
                window[c, z, t * YREACH:(t + 1) * YREACH, :] = tile_of(c, t).astype(jnp.float32)

    def widen_home(z, _):
        widen(z, lambda c, t: field[home, side, t, c, z], range(1, last))
        return 0

    lax.fori_loop(0, planes, widen_home, 0)

    def fill_home(m, _):
        for z in range(deep):
            for c in range(3):
                block = window[c, m * deep + z, YREACH:YREACH + rows, :].astype(jnp.bfloat16)
                at = c * high_rows + z * rows
                for buffer in range(2):
                    matrix[buffer, m, at:at + rows, length:] = block
        out_ref[pl.ds(m * deep, deep)] = jnp.zeros((deep, rows, length), jnp.float32)
        return 0

    lax.fori_loop(0, strips, fill_home, 0)

    def end_plane(slot):
        return lambda lag, z: (lambda c, t: field[slot, side, t, c, z])

    def any_plane(lag, z):
        away = lag_ref[2, lag] + z + 2 * reach * planes
        block = lax.div(away, planes) + side
        place = lax.rem(away, planes)
        parity = lax.rem(block, 2)
        if paired:
            slot = lax.rem(pair + lax.div(block, 2) + pairs - reach % pairs, pairs) ^ pair
        else:
            slot = lax.rem(lax.div(block, 2), pairs)
        return lambda c, t: field[slot, parity, t, c, place]

    def sweep(work, ahead_work, buffer):
        def strip(m, _):
            if ahead_work is not None:
                later, plane_of = ahead_work
                turn = lax.rem(length - lag_ref[0, later], length)
                lag_y = lag_ref[1, later]
                for z in range(deep):
                    widen(m * deep + z, plane_of(later, m * deep + z), range(last + 1))
                for z in range(deep):
                    for c in range(3):
                        block = window[c, m * deep + z, pl.ds(YREACH + lag_y, rows), :]
                        at = c * high_rows + z * rows
                        matrix[1 - buffer, m, at:at + rows, :length] = pltpu.roll(block, turn, 1).astype(jnp.bfloat16)
            if work is not None:
                total = out_ref[pl.ds(m * deep, deep)].reshape(high_rows, length)
                for q in range(NOFF // 2):
                    pieces = jnp.dot(matrix[buffer, m], shifts[q], preferred_element_type=jnp.float32)
                    for h in range(2):
                        row = index_ref[work, 2 * q + h]
                        g = [weight_ref[c, row] for c in range(3)]
                        diff = [
                            pieces[c * high_rows:(c + 1) * high_rows, h * length:(h + 1) * length]
                            for c in range(3)
                        ]
                        along = g[0] * diff[0] + g[1] * diff[1] + g[2] * diff[2]
                        energy = diff[0] * diff[0] + diff[1] * diff[1] + diff[2] * diff[2]
                        total = total + along * energy
                out_ref[pl.ds(m * deep, deep)] = total.reshape(deep, rows, length)
            return 0

        lax.fori_loop(0, strips, strip, 0)

    def pass_halo(s, edge):
        halos[s, edge].wait_recv()
        go(share(field.at[s, side, edge], s, edge))

    plus = jnp.int32(0)
    minus = jnp.int32(0)
    for lag in range(NLAG - 1, -1, -1):
        plus = jnp.where(lag_ref[2, lag] == REACH, lag, plus)
        minus = jnp.where(lag_ref[2, lag] == -REACH, lag, minus)

    def pass_main(s, t):
        mains[s, t].wait_recv()
        if t == 0:
            halos[s, last] = go(direct(field.at[s, side, 1], s, last, (me, down)))
        if t == tiles - 1:
            halos[s, 0] = go(direct(field.at[s, side, tiles], s, 0, (me, up)))
        if relayed and t in relayed[s]:
            mains[far[0], t] = go(direct(field.at[s, side, t + 1], far[0], t + 1, peer(far[0] ^ s)))
        go(share(field.at[s, side, t + 1], s, t + 1))

    for t in order[:2]:
        for s in near:
            pass_main(s, t)
    for edge in (last, 0):
        pass_halo(home, edge)
        for s in far:
            halos[s, edge] = go(direct(field.at[home, side, edge], s, edge, peer(s)))
    for t in order[2:]:
        for s in near:
            pass_main(s, t)
    early = [ahead] if ahead == behind else near
    for s in early:
        for edge in (last, 0):
            pass_halo(s, edge)
    sweep(None, (plus, end_plane(ahead)), 1)
    sweep(plus, (minus, end_plane(behind)), 0)
    for s in far:
        for t in order:
            mains[s, t].wait_recv()
            go(share(field.at[s, side, t + 1], s, t + 1))
    for s in near:
        if s not in early:
            for edge in (last, 0):
                pass_halo(s, edge)
    sweep(minus, None, 1)
    for s in far:
        for edge in (last, 0):
            pass_halo(s, edge)
    for s in [home] + others:
        for t in range(last + 1):
            incoming(s, t).wait_recv()

    low = jnp.minimum(plus, minus)
    high = jnp.maximum(plus, minus)

    rest = []
    for j in range(NLAG - 2):
        lag = j + jnp.where(j >= low, 1, 0)
        rest.append((lag + jnp.where(lag >= high, 1, 0), any_plane))
    for j, work in enumerate([None] + rest):
        sweep(None if work is None else work[0], rest[j] if j < len(rest) else None, (j + 1) % 2)

    def finish(z, _):
        out_ref[z] = out_ref[z] * (0.25 / (NLAG * NOFF))
        return 0

    lax.fori_loop(0, planes, finish, 0)
    for copy in started:
        copy.wait_send()


def solution(mesh):
    count = mesh.shape["gz"]
    columns = mesh.shape["gy"]
    pairs = count // 2

    def per_device(velocity, lag_table, filter_index, filter_weights):
        parts, planes, rows, length = velocity.shape
        reach = REACH // (2 * planes)
        tiles = rows // YREACH
        strips = max(1, planes * rows // 64)
        slots = min(pairs, 2 * reach + 1)
        blocks = velocity.reshape(parts, planes, tiles, YREACH, length)
        smem = pl.BlockSpec(memory_space=pltpu.SMEM)
        return pl.pallas_call(
            functools.partial(kernel, pairs, reach, columns),
            out_shape=jax.ShapeDtypeStruct((planes, rows, length), jnp.float32),
            in_specs=[smem, smem, smem, pl.BlockSpec(memory_space=pl.ANY)],
            out_specs=pl.BlockSpec(memory_space=pltpu.VMEM),
            scratch_shapes=[
                pltpu.VMEM((slots, 2, tiles + 2, parts, planes, YREACH, length), jnp.bfloat16),
                pltpu.VMEM((parts, planes, rows + 2 * YREACH, length), jnp.float32),
                pltpu.VMEM((2, strips, parts * planes * rows // strips, 2 * length), jnp.bfloat16),
                pltpu.VMEM((NOFF // 2, 2 * length, 2 * length), jnp.bfloat16),
                pltpu.SemaphoreType.DMA((tiles,)),
                pltpu.SemaphoreType.DMA((slots, tiles + 2)),
                pltpu.SemaphoreType.DMA((slots, tiles + 2)),
                pltpu.SemaphoreType.DMA((slots, tiles + 2)),
                pltpu.SemaphoreType.DMA((slots, tiles + 2)),
            ],
            compiler_params=pltpu.CompilerParams(collective_id=0, has_side_effects=True),
        )(lag_table.T, filter_index, filter_weights, blocks)

    return jax.shard_map(
        per_device,
        mesh=mesh,
        in_specs=(P(None, "gz", "gy", None), P(), P(), P()),
        out_specs=P("gz", "gy", None),
        check_vma=False,
    )
```

```python
import functools

import jax
import jax.numpy as jnp
from jax import lax
from jax.experimental import pallas as pl
from jax.experimental.pallas import tpu as pltpu
from jax.sharding import PartitionSpec as P

NLAG = 5
NOFF = 16
REACH = 64
YREACH = 4
MESH = pl.DeviceIdType.MESH


def kernel(
    pairs, reach, columns, lag_ref, index_ref, weight_ref, vel_ref, out_ref,
    field, window, matrix, shifts, own_sem, send_sem, recv_sem, share_send, share_recv
):
    planes, tiles = vel_ref.shape[1], vel_ref.shape[2]
    length = vel_ref.shape[4]
    slots = field.shape[0]
    rows = out_ref.shape[1]
    strips = matrix.shape[1]
    deep = planes // strips
    high_rows = deep * rows
    order = [0, tiles - 1] + list(range(1, tiles - 1))
    last = tiles + 1
    me = lax.axis_index("gz")
    col = lax.axis_index("gy")
    pair = me // 2
    side = lax.rem(me, 2)
    up = lax.rem(col + 1, columns)
    down = lax.rem(col + columns - 1, columns)
    partner = (pair * 2 + 1 - side, col)

    paired = slots == pairs and pairs & (pairs - 1) == 0 and reach % pairs in (0, pairs // 2)
    if paired:
        home = 0
        ahead = behind = reach % pairs
        others = sorted(range(1, slots), key=lambda s: (bin(s).count("1"), s != ahead))
        far = [s for s in others if bin(s).count("1") > 1]
    else:
        home, ahead, behind = reach % pairs, (2 * reach) % pairs, 0
        others = sorted((s for s in range(slots) if s != home), key=lambda s: -abs(s - reach))
        far = []
    near = [s for s in others if s not in far]
    relayed = None
    if len(far) == 1 and len(near) == 2:
        relayed = {near[0]: range(tiles // 2), near[1]: range(tiles // 2, tiles)}

    def peer(slot):
        if paired:
            other = pair
            for bit in range(pairs.bit_length()):
                if slot >> bit & 1:
                    other = other + (1 << bit) - (2 << bit) * lax.rem(pair // (1 << bit), 2)
        else:
            other = lax.rem(pair + pairs + reach - slot, pairs)
        return (other * 2 + side, col)

    own = [
        pltpu.make_async_copy(vel_ref.at[:, :, t], field.at[home, side, t + 1], own_sem.at[t])
        for t in order
    ]
    for copy in own:
        copy.start()

    barrier = pltpu.get_barrier_semaphore()
    greeted = [peer(s) for s in others] + [partner, (me, up), (me, down)]
    for device in greeted:
        pl.semaphore_signal(barrier, inc=1, device_id=device, device_id_type=MESH)
    pl.semaphore_wait(barrier, len(greeted))

    def direct(src, slot, tile, device):
        return pltpu.make_async_remote_copy(
            src_ref=src,
            dst_ref=field.at[slot, side, tile],
            send_sem=send_sem.at[slot, tile],
            recv_sem=recv_sem.at[slot, tile],
            device_id=device,
            device_id_type=MESH,
        )

    def share(src, slot, tile):
        return pltpu.make_async_remote_copy(
            src_ref=src,
            dst_ref=field.at[slot, side, tile],
            send_sem=share_send.at[slot, tile],
            recv_sem=share_recv.at[slot, tile],
            device_id=partner,
            device_id_type=MESH,
        )

    def incoming(slot, tile):
        return pltpu.make_async_remote_copy(
            src_ref=field.at[slot, 1 - side, tile],
            dst_ref=field.at[slot, 1 - side, tile],
            send_sem=share_send.at[slot, tile],
            recv_sem=share_recv.at[slot, tile],
            device_id=partner,
            device_id_type=MESH,
        )

    started = []

    def go(copy):
        copy.start()
        started.append(copy)
        return copy

    for copy in own:
        copy.wait()
    mains = {}
    halos = {}
    halos[home, 0] = go(direct(field.at[home, side, tiles], home, 0, (me, up)))
    halos[home, last] = go(direct(field.at[home, side, 1], home, last, (me, down)))
    for t in order:
        for s in near if relayed else others:
            mains[s, t] = go(direct(field.at[home, side, t + 1], s, t + 1, peer(s)))
    for t in order:
        go(share(field.at[home, side, t + 1], home, t + 1))

    def build(q, _):
        source = lax.broadcasted_iota(jnp.int32, (length, 2 * length), 0)
        column = lax.broadcasted_iota(jnp.int32, (length, 2 * length), 1)
        point = lax.rem(column, length)
        wanted = lax.rem(point + 2 * q + lax.div(column, length), length)
        shifts[q, :length, :] = jnp.where(source == wanted, 1.0, 0.0).astype(jnp.bfloat16)
        shifts[q, length:, :] = jnp.where(source == point, -1.0, 0.0).astype(jnp.bfloat16)
        return 0

    lax.fori_loop(0, NOFF // 2, build, 0)

    def widen(z, tile_of, groups):
        for c in range(3):
            for t in groups:
                window[c, z, t * YREACH:(t + 1) * YREACH, :] = tile_of(c, t).astype(jnp.float32)

    def widen_home(z, _):
        widen(z, lambda c, t: field[home, side, t, c, z], range(1, last))
        return 0

    lax.fori_loop(0, planes, widen_home, 0)

    def fill_home(m, _):
        for z in range(deep):
            for c in range(3):
                block = window[c, m * deep + z, YREACH:YREACH + rows, :].astype(jnp.bfloat16)
                at = c * high_rows + z * rows
                for buffer in range(2):
                    matrix[buffer, m, at:at + rows, length:] = block
        out_ref[pl.ds(m * deep, deep)] = jnp.zeros((deep, rows, length), jnp.float32)
        return 0

    lax.fori_loop(0, strips, fill_home, 0)

    def end_plane(slot):
        return lambda lag, z: (lambda c, t: field[slot, side, t, c, z])

    def any_plane(lag, z):
        away = lag_ref[2, lag] + z + 2 * reach * planes
        block = lax.div(away, planes) + side
        place = lax.rem(away, planes)
        parity = lax.rem(block, 2)
        if paired:
            slot = lax.rem(pair + lax.div(block, 2) + pairs - reach % pairs, pairs) ^ pair
        else:
            slot = lax.rem(lax.div(block, 2), pairs)
        return lambda c, t: field[slot, parity, t, c, place]

    def sweep(work, ahead_work, buffer, scale=None):
        def strip(m, _):
            if ahead_work is not None:
                later, plane_of = ahead_work
                turn = lax.rem(length - lag_ref[0, later], length)
                lag_y = lag_ref[1, later]
                for z in range(deep):
                    widen(m * deep + z, plane_of(later, m * deep + z), range(last + 1))
                for z in range(deep):
                    for c in range(3):
                        block = window[c, m * deep + z, pl.ds(YREACH + lag_y, rows), :]
                        at = c * high_rows + z * rows
                        matrix[1 - buffer, m, at:at + rows, :length] = pltpu.roll(block, turn, 1).astype(jnp.bfloat16)
            if work is not None:
                total = out_ref[pl.ds(m * deep, deep)].reshape(high_rows, length)
                for q in range(NOFF // 2):
                    pieces = jnp.dot(matrix[buffer, m], shifts[q], preferred_element_type=jnp.float32)
                    for h in range(2):
                        row = index_ref[work, 2 * q + h]
                        g = [weight_ref[c, row] for c in range(3)]
                        diff = [
                            pieces[c * high_rows:(c + 1) * high_rows, h * length:(h + 1) * length]
                            for c in range(3)
                        ]
                        along = g[0] * diff[0] + g[1] * diff[1] + g[2] * diff[2]
                        energy = diff[0] * diff[0] + diff[1] * diff[1] + diff[2] * diff[2]
                        total = total + along * energy
                if scale is not None:
                    total = total * scale
                out_ref[pl.ds(m * deep, deep)] = total.reshape(deep, rows, length)
            return 0

        lax.fori_loop(0, strips, strip, 0)

    def pass_halo(s, edge):
        halos[s, edge].wait_recv()
        go(share(field.at[s, side, edge], s, edge))

    plus = jnp.int32(0)
    minus = jnp.int32(0)
    for lag in range(NLAG - 1, -1, -1):
        plus = jnp.where(lag_ref[2, lag] == REACH, lag, plus)
        minus = jnp.where(lag_ref[2, lag] == -REACH, lag, minus)

    def pass_main(s, t):
        mains[s, t].wait_recv()
        if t == 0:
            halos[s, last] = go(direct(field.at[s, side, 1], s, last, (me, down)))
        if t == tiles - 1:
            halos[s, 0] = go(direct(field.at[s, side, tiles], s, 0, (me, up)))
        if relayed and t in relayed[s]:
            mains[far[0], t] = go(direct(field.at[s, side, t + 1], far[0], t + 1, peer(far[0] ^ s)))
        go(share(field.at[s, side, t + 1], s, t + 1))

    for t in order[:2]:
        for s in near:
            pass_main(s, t)
    for edge in (last, 0):
        pass_halo(home, edge)
        for s in far:
            halos[s, edge] = go(direct(field.at[home, side, edge], s, edge, peer(s)))
    for t in order[2:]:
        for s in near:
            pass_main(s, t)
    early = [ahead] if ahead == behind else near
    for s in early:
        for edge in (last, 0):
            pass_halo(s, edge)
    sweep(None, (plus, end_plane(ahead)), 1)
    sweep(plus, (minus, end_plane(behind)), 0)
    for s in far:
        for t in order:
            mains[s, t].wait_recv()
            go(share(field.at[s, side, t + 1], s, t + 1))
    for s in near:
        if s not in early:
            for edge in (last, 0):
                pass_halo(s, edge)
    for s in far:
        for edge in (last, 0):
            pass_halo(s, edge)
    sweep(minus, None, 1)
    for s in [home] + others:
        for t in range(last + 1):
            incoming(s, t).wait_recv()

    low = jnp.minimum(plus, minus)
    high = jnp.maximum(plus, minus)

    rest = []
    for j in range(NLAG - 2):
        lag = j + jnp.where(j >= low, 1, 0)
        rest.append((lag + jnp.where(lag >= high, 1, 0), any_plane))
    for j, work in enumerate([None] + rest):
        scale = 0.25 / (NLAG * NOFF) if j == len(rest) else None
        sweep(None if work is None else work[0], rest[j] if j < len(rest) else None, (j + 1) % 2, scale)

    for copy in started:
        copy.wait_send()


def solution(mesh):
    count = mesh.shape["gz"]
    columns = mesh.shape["gy"]
    pairs = count // 2

    def per_device(velocity, lag_table, filter_index, filter_weights):
        parts, planes, rows, length = velocity.shape
        reach = REACH // (2 * planes)
        tiles = rows // YREACH
        strips = max(1, planes * rows // 64)
        slots = min(pairs, 2 * reach + 1)
        blocks = velocity.reshape(parts, planes, tiles, YREACH, length)
        smem = pl.BlockSpec(memory_space=pltpu.SMEM)
        return pl.pallas_call(
            functools.partial(kernel, pairs, reach, columns),
            out_shape=jax.ShapeDtypeStruct((planes, rows, length), jnp.float32),
            in_specs=[smem, smem, smem, pl.BlockSpec(memory_space=pl.ANY)],
            out_specs=pl.BlockSpec(memory_space=pltpu.VMEM),
            scratch_shapes=[
                pltpu.VMEM((slots, 2, tiles + 2, parts, planes, YREACH, length), jnp.bfloat16),
                pltpu.VMEM((parts, planes, rows + 2 * YREACH, length), jnp.float32),
                pltpu.VMEM((2, strips, parts * planes * rows // strips, 2 * length), jnp.bfloat16),
                pltpu.VMEM((NOFF // 2, 2 * length, 2 * length), jnp.bfloat16),
                pltpu.SemaphoreType.DMA((tiles,)),
                pltpu.SemaphoreType.DMA((slots, tiles + 2)),
                pltpu.SemaphoreType.DMA((slots, tiles + 2)),
                pltpu.SemaphoreType.DMA((slots, tiles + 2)),
                pltpu.SemaphoreType.DMA((slots, tiles + 2)),
            ],
            compiler_params=pltpu.CompilerParams(collective_id=0, has_side_effects=True),
        )(lag_table.T, filter_index, filter_weights, blocks)

    return jax.shard_map(
        per_device,
        mesh=mesh,
        in_specs=(P(None, "gz", "gy", None), P(), P(), P()),
        out_specs=P("gz", "gy", None),
        check_vma=False,
    )
```
